256 devices in a mesh: group: 16 (over z, core), helper: 16 (over y, x).
Axes of the slice: x: 4, y: 4, z: 8, core: 2. Of those that a mesh axis runs over, the one named last changes fastest.
Arguments:
- candidates: bfloat16 [2048, 128, 1024], P(('group', 'helper')), may hold values from -36 to 36
- block_user: int32 [2048], P(('group', 'helper')), may hold values from 0 to 15, as said below
- live_rows: int32 [2048], P(('group', 'helper')), may hold values from 1 to 128
- prefix_keys: bfloat16 [256, 256, 1024], P(('group', 'helper')), may hold values from -6 to 6
- prefix_values: bfloat16 [256, 256, 1024], P(('group', 'helper')), may hold values from -6 to 6
- w_proj: bfloat16 [1024, 4096], P(('group', 'helper')), may hold values from -0.1875 to 0.1875
- w_out: bfloat16 [1024, 1024], P(('group', 'helper')), may hold values from -0.1875 to 0.1875
- gain_in: float32 [1024], replicated, may hold values from 0.1 to 1.9
- gain_mid: float32 [1024], replicated, may hold values from 0.1 to 1.9
- score_vec: float32 [1024], replicated, may hold values from -0.1875 to 0.1875
Outputs:
- embeddings: bfloat16 [2048, 128, 1024], P(('group', 'helper'))
- scores: float32 [2048, 128], P(('group', 'helper'))
The draws below stay inside these ranges and needn't reach their ends.
Inputs may be any that keep to these rules, and one draw needn't show every extreme that they name: `block_user`: the 8 blocks of one device name different users; in every group some user is named by a block of every device of the group.
All inputs are finite; a program needn't handle non-finite values.
Results may differ from the reference program's by a relative error of at most 0.0045.
Values may be sent and summed in bfloat16 or wider, within the bound.
A program may use at most 128 MiB of HBM per device.

```python
import math
import jax
import jax.numpy as jnp
from jax import lax

D = 1024
HEADS = 8
ROWS = 128
PREFIX = 256
BLK_DEV = 8
BLOCKS = 2048
USERS = 256
N_GROUP = 16
N_HELPER = 16


def assignment(key):
    base_key = jax.random.fold_in(key, 7)
    key_hot, key_rank, key_place, key_live = jax.random.split(base_key, 4)
    device_count = N_GROUP * N_HELPER
    hot_user = jax.random.randint(key_hot, (N_GROUP, 1), 0, N_HELPER).astype(jnp.int32)
    hot_device = jnp.repeat(hot_user, N_HELPER, axis=0)
    rank_keys = jax.random.split(key_rank, device_count)
    rank_table = jax.vmap(lambda piece_key: jax.random.permutation(piece_key, N_HELPER))(rank_keys).astype(jnp.int32)
    user_ids = jnp.arange(N_HELPER, dtype=jnp.int32)[None, :]
    rank_table = jnp.where(user_ids == hot_device, -1, rank_table)
    ordering = jnp.argsort(rank_table, axis=1, stable=True).astype(jnp.int32)
    chosen = ordering[:, :BLK_DEV]
    place_keys = jax.random.split(key_place, device_count)
    positions = jax.vmap(lambda piece_key: jax.random.permutation(piece_key, BLK_DEV))(place_keys).astype(jnp.int32)
    chosen = jnp.take_along_axis(chosen, positions, axis=1)
    lives = jax.random.randint(key_live, (device_count, BLK_DEV), 1, ROWS + 1).astype(jnp.int32)
    lives = jnp.where(chosen == hot_device, ROWS, lives)
    return (chosen.reshape(-1).astype(jnp.int32), lives.reshape(-1).astype(jnp.int32))


def draw_block_user(key, part):
    return assignment(key)[0]


def draw_live_rows(key, part):
    return assignment(key)[1]


def draw_candidates(key, part):
    base_key = jax.random.fold_in(key, 11)
    key_base, key_row, key_col = jax.random.split(base_key, 3)
    dims_full = (BLOCKS, ROWS, D)
    row_scale = jnp.exp(jax.random.uniform(key_row, (BLOCKS, ROWS, 1), jnp.float32, math.log(0.3), math.log(3.0)))
    col_scale = jnp.exp(jax.random.uniform(key_col, (1, 1, D), jnp.float32, math.log(0.3), math.log(3.0)))
    base_draw = jnp.clip(jax.random.normal(key_base, dims_full, jnp.float32), -4.0, 4.0)
    return (base_draw * row_scale * col_scale).astype(jnp.bfloat16)


def steps_of(own_key, extent, shards, smallest, top_value):
    level, own = 1.0, jax.random.fold_in(own_key, 6)
    for axis_at, parts in shards:
        draws = jnp.exp(jax.random.uniform(jax.random.fold_in(own, axis_at), (parts,), jnp.float32, smallest / len(shards), top_value / len(shards)))
        level = level * jnp.repeat(draws, extent[axis_at] // parts).reshape([-1 if axis == axis_at else 1 for axis in range(len(extent))])
    return level


def scatter_about(rng, shape, scale, most, cuts=(), kind=jnp.bfloat16):
    drawn = scale * jax.random.normal(rng, shape, jnp.float32)
    if cuts:
        drawn = drawn * steps_of(rng, shape, cuts, -0.22, 0.18)
    return jnp.clip(drawn, -most, most).astype(kind)


def setup_inputs(seed: int = 0) -> dict:
    streams_of = jax.random.split(jax.random.key(seed), 11)
    candidates = draw_candidates(jax.random.fold_in(streams_of[10], 71), 0)
    block_user = draw_block_user(jax.random.fold_in(streams_of[10], 71), 0)
    live_rows = draw_live_rows(jax.random.fold_in(streams_of[10], 71), 0)
    prefix_keys = scatter_about(streams_of[3], (USERS, PREFIX, D), 1.0, 6.0, ((0, 256),))
    prefix_values = scatter_about(streams_of[4], (USERS, PREFIX, D), 1.0, 6.0, ((0, 256),))
    w_proj = scatter_about(streams_of[5], (D, 4 * D), D ** -0.5, 0.1875, ((0, 256),))
    w_out = scatter_about(streams_of[6], (D, D), D ** -0.5, 0.1875, ((0, 256),))
    gain_in = jnp.clip(1.0 + 0.18 * jax.random.normal(streams_of[7], (D,), jnp.float32), 0.1, 1.9)
    gain_mid = jnp.clip(1.0 + 0.18 * jax.random.normal(streams_of[8], (D,), jnp.float32), 0.1, 1.9)
    score_vec = scatter_about(streams_of[9], (D,), D ** -0.5, 0.1875, (), jnp.float32)
    return dict(candidates=candidates, block_user=block_user, live_rows=live_rows, prefix_keys=prefix_keys, prefix_values=prefix_values, w_proj=w_proj, w_out=w_out, gain_in=gain_in, gain_mid=gain_mid, score_vec=score_vec)


epsilon = 1e-05

def layer_norm(values, gain):
    average = lax.optimization_barrier(jnp.mean(values, axis=-1, keepdims=True))
    centred = values - average
    spread = lax.optimization_barrier(jnp.mean(centred * centred, axis=-1, keepdims=True))
    return centred * lax.rsqrt(spread + epsilon) * gain

def reference(candidates, block_user, live_rows, prefix_keys, prefix_values, w_proj, w_out, gain_in, gain_mid, score_vec):
    head_dim = D // HEADS
    score_scale = head_dim ** (-0.5)
    device_count = N_GROUP * N_HELPER
    owners_all = jnp.arange(BLOCKS, dtype=jnp.int32) // (BLK_DEV * N_HELPER) * N_HELPER + block_user.astype(jnp.int32)
    grouped = (candidates.reshape(device_count, BLK_DEV, ROWS, D), owners_all.reshape(device_count, BLK_DEV), live_rows.reshape(device_count, BLK_DEV))

    def one_device(inputs):
        cand_blocks, owners, lives = inputs
        cand_rows = cand_blocks.reshape(BLK_DEV * ROWS, D).astype(jnp.float32)
        normed = layer_norm(cand_rows, gain_in).astype(jnp.bfloat16)
        projected = jax.nn.silu(jnp.dot(normed, w_proj, preferred_element_type=jnp.float32))
        gate_portion = projected[:, :D]
        value_part = projected[:, D:2 * D]
        query_portion = projected[:, 2 * D:3 * D]
        key_part = projected[:, 3 * D:]
        query_bf = lax.optimization_barrier(query_portion.astype(jnp.bfloat16))
        query_heads = query_bf.astype(jnp.float32).reshape(-1, HEADS, head_dim)
        own_weight = jax.nn.silu(score_scale * lax.optimization_barrier(jnp.sum(query_heads * key_part.reshape(-1, HEADS, head_dim), axis=-1)))
        own_term = (own_weight[..., None] * value_part.reshape(-1, HEADS, head_dim)).reshape(-1, D)
        key_sel = jnp.take(prefix_keys, owners, axis=0).astype(jnp.float32).reshape(BLK_DEV, PREFIX, HEADS, head_dim)
        selected_values = jnp.take(prefix_values, owners, axis=0).astype(jnp.float32).reshape(BLK_DEV, PREFIX, HEADS, head_dim)
        query_blocks = query_heads.reshape(BLK_DEV, ROWS, HEADS, head_dim)
        raw_scores = jnp.einsum('brhd,bphd->bhrp', query_blocks, key_sel)
        weight_brainfloat = lax.optimization_barrier(jax.nn.silu(score_scale * raw_scores).astype(jnp.bfloat16))
        prefix_mix = jnp.einsum('bhrp,bphd->brhd', weight_brainfloat.astype(jnp.float32), selected_values)
        prefix_bf = lax.optimization_barrier(prefix_mix.astype(jnp.bfloat16))
        mixed = prefix_bf.astype(jnp.float32).reshape(-1, D) + own_term
        gated = (layer_norm(mixed, gain_mid) * gate_portion).astype(jnp.bfloat16)
        updated = cand_rows + jnp.dot(gated, w_out, preferred_element_type=jnp.float32)
        embedded = updated.astype(jnp.bfloat16).reshape(BLK_DEV, ROWS, D)
        row_scores = lax.optimization_barrier(jnp.sum(layer_norm(updated, 1.0) * score_vec, axis=-1)).reshape(BLK_DEV, ROWS)
        live_mask = jnp.arange(ROWS, dtype=jnp.int32)[None, :] < lives[:, None]
        return (embedded, jnp.where(live_mask, row_scores, jnp.zeros_like(row_scores)))
    embedded_all, scores_all = lax.map(one_device, grouped)
    return (embedded_all.reshape(BLOCKS, ROWS, D), scores_all.reshape(BLOCKS, ROWS))
```

```python
import functools

import jax
import jax.numpy as jnp
from jax import lax
from jax.experimental import pallas as pl
from jax.experimental.pallas import tpu as pltpu
from jax.sharding import PartitionSpec as P

MESH = pl.DeviceIdType.MESH
HEADS = 8
EPS = 1e-05
CHUNKS = 4
HOLD = ((0, 0), (0, 1), (1, 0), (0, 2), (2, 0), (2, 3))
PARENT = (None, 0, 0, 1, 2, 4)
LEVELS = ((1, 2), (3, 4), (5,))


def split_others():
    ways = ((0, 1), (0, 3), (1, 0), (3, 0))
    groups = {way: [] for way in ways}
    rest = []
    for y in range(4):
        for x in range(4):
            if (y, x) not in HOLD:
                near = {w: (((y + w[0]) % 4), (x + w[1]) % 4) for w in ways}
                rest.append([(w, HOLD.index(n)) for w, n in near.items() if n in HOLD])
    for options in sorted(rest, key=len):
        way, held = min(options, key=lambda o: len(groups[o[0]]))
        groups[way].append(held)
    return tuple((way, tuple(held)) for way, held in groups.items() if held)


GROUPS = split_others()
STARTS = tuple(sum(len(h) for _, h in GROUPS[:k]) for k in range(len(GROUPS)))
SENT = tuple((way, held) for way, helds in GROUPS for held in helds)
HERE = len(HOLD)
PAIRS = HERE + len(SENT)


def turn(offset, c):
    dy, dx = offset
    even, odd = (1 - c % 2) * (1 - c), (c % 2) * (2 - c)
    return even * dy + odd * dx, even * dx - odd * dy


def silu(v):
    half = 0.5 * v
    return half + half * jnp.tanh(half)


def centred(v):
    v = v - jnp.mean(v, axis=-1, keepdims=True)
    return v * lax.rsqrt(jnp.mean(v * v, axis=-1, keepdims=True) + EPS)


def kernel(
    cand, users, live, keys, values, w_proj, w_out, gain_in, gain_mid, score_vec,
    emb, scores,
    xb, normed, wraw, wfull, kv, q, own, gate, qs, qr, res, mix, block_of, place_of,
    loc, w1s, w1r, zs, zr, ps, pr, ks, kr, qss, qrs, rss, rrs,
):
    g, h = lax.axis_index("group"), lax.axis_index("helper")
    z, core = g // 2, g % 2
    y, x = h // 4, h % 4
    blocks, rows, width = xb.shape
    part = wraw.shape[2] // 5
    cols = width // CHUNKS
    alpha = (width // HEADS) ** -0.5

    def plane(offset):
        return lax.rem(y + offset[0] + 8, 4) * 4 + lax.rem(x + offset[1] + 8, 4)

    def along(step):
        return lax.rem(z + step + 8, 8)

    local = [
        pltpu.make_async_copy(w_proj, wraw.at[h, :, pl.ds(0, 4 * part)], loc.at[0]),
        pltpu.make_async_copy(w_out, wraw.at[h, :, pl.ds(4 * part, part)], loc.at[1]),
        pltpu.make_async_copy(cand, xb, loc.at[2]),
    ]
    for c in range(CHUNKS):
        for k, src in enumerate((keys, values)):
            local.append(
                pltpu.make_async_copy(
                    src.at[0, :, pl.ds(c * cols, cols)],
                    kv.at[c, 0, pl.ds(k * 256, 256)],
                    loc.at[3 + 2 * c + k],
                )
            )
    for copy in local:
        copy.start()

    barrier = pltpu.get_barrier_semaphore()
    peers = [(g, lax.rem(h + k, 16)) for k in range(1, 16)]
    peers += [(2 * along(1) + core, h), (2 * along(-1) + core, h), (2 * z + 1 - core, h)]
    for peer in peers:
        pl.semaphore_signal(barrier, inc=1, device_id=peer, device_id_type=MESH)
    pl.semaphore_wait(barrier, len(peers))

    sent = []

    def send(src, dst, s, r, device):
        copy = pltpu.make_async_remote_copy(
            src_ref=src, dst_ref=dst, send_sem=s, recv_sem=r, device_id=device, device_id_type=MESH
        )
        copy.start()
        return copy

    local[0].wait()
    local[1].wait()

    def w1(k, at):
        return pltpu.make_async_remote_copy(
            src_ref=wraw.at[at], dst_ref=wraw.at[at], send_sem=w1s.at[k], recv_sem=w1r.at[k],
            device_id=(g, lax.rem(h + k, 16)), device_id_type=MESH,
        )

    for k in range(1, 16):
        copy = w1(k, h)
        copy.start()
        sent.append(copy)

    def kv_send(c, child):
        parent = PARENT[child]
        a, b = HOLD[parent], HOLD[child]
        step = turn((b[0] - a[0], b[1] - a[1]), c)
        step = tuple((s + 2) % 4 - 2 if s not in (2, -2) else s for s in step)
        return pltpu.make_async_remote_copy(
            src_ref=kv.at[c, parent], dst_ref=kv.at[c, child], send_sem=ks.at[c, child],
            recv_sem=kr.at[c, child], device_id=(g, plane(step)), device_id_type=MESH,
        )

    def kv_level(level, after):
        for c in range(CHUNKS):
            if level == 0:
                local[3 + 2 * c].wait()
                local[4 + 2 * c].wait()
            for child in LEVELS[level]:
                if PARENT[child]:
                    kv_send(c, PARENT[child]).wait_recv()
                copy = kv_send(c, child)
                copy.start()
                sent.append(copy)

    kv_level(0, None)

    for u in range(16):
        found = jnp.int32(0)
        for b in range(blocks):
            found = jnp.where(users[b] == u, jnp.int32(b), found)
        block_of[u] = found

    def user_of(c, p):
        if p < HERE:
            dy, dx = turn(HOLD[p], c)
            return plane((-dy, -dx))
        way, held = SENT[p - HERE]
        dy, dx = turn((way[0] - HOLD[held][0], way[1] - HOLD[held][1]), c)
        return plane((dy, dx))

    for c in range(CHUNKS):
        for p in range(PAIRS):
            place_of[c * 16 + user_of(c, p)] = jnp.int32(p)

    local[2].wait()

    @pl.loop(0, blocks)
    def _(b):
        v = centred(xb[b].astype(jnp.float32)) * gain_in[...]
        normed[pl.ds(pl.multiple_of(b * rows, rows), rows), :] = v.astype(jnp.bfloat16)

    def slab(at, of_core):
        return pl.ds(pl.multiple_of((2 * at + of_core) * 64, 64), 64)

    def z_copy(j, t, unit, way, at):
        ref = wfull.at[j, slab(at, core), pl.ds(unit * (part // 2), part // 2)]
        where = (t * 2 + unit) * 2 + way
        return pltpu.make_async_remote_copy(
            src_ref=ref, dst_ref=ref, send_sem=zs.at[j, where], recv_sem=zr.at[j, where],
            device_id=(2 * along(1 - 2 * way) + core, h), device_id_type=MESH,
        )

    def p_copy(j, n, at, of_core):
        ref = wfull.at[j, slab(at, of_core)]
        return pltpu.make_async_remote_copy(
            src_ref=ref, dst_ref=ref, send_sem=ps.at[j, n], recv_sem=pr.at[j, n],
            device_id=(2 * z + 1 - core, h), device_id_type=MESH,
        )

    def z_own(j):
        for unit in range(2):
            for way in range(2):
                z_copy(j, 0, unit, way, z).start()
        p_copy(j, 0, z, core).start()

    def tick(j, t):
        left, right = along(-1 - t), lax.rem(z + 1 + t, 8)
        for unit in range(2):
            for way in range(2):
                at = (left, right)[way]

                def step(last):
                    z_copy(j, t, unit, way, at).wait_recv()

                    @pl.when(t < last)
                    def _():
                        z_copy(j, t + 1, unit, way, at).start()

                if unit == way:
                    step(3)
                else:
                    pl.when(t < 3)(functools.partial(step, 2))
        p_copy(j, 1 + 2 * t, left, core).start()

        @pl.when(t < 3)
        def _():
            p_copy(j, 2 + 2 * t, right, core).start()

        if j < 4:

            @pl.when(t == 2)
            def _():
                z_own(j + 1)

    def p_wait(j):
        p_copy(j, 0, z, 1 - core).wait_recv()

        @pl.loop(0, 4)
        def _(t):
            p_copy(j, 1 + 2 * t, along(-1 - t), 1 - core).wait_recv()

            @pl.when(t < 3)
            def _():
                p_copy(j, 2 + 2 * t, lax.rem(z + 1 + t, 8), 1 - core).wait_recv()

    ORDER = (2, 3, 1, 0, 4)

    for k in range(1, 16):
        w1(k, lax.rem(h - k + 16, 16)).wait_recv()
    for j in range(5):
        piece = wraw[:, :, pl.ds(ORDER[j] * part, part)]
        wfull[j, slab(z, core), :] = piece.reshape(64, part)
    z_own(0)

    def projected(j, t):
        at = pl.ds(pl.multiple_of(t * 256, 256), 256)
        return at, silu(jnp.dot(normed[at, :], wfull[j], preferred_element_type=jnp.float32))

    def tile_q(t):
        _, v = projected(0, t)
        v = v.astype(jnp.bfloat16)
        for c in range(CHUNKS):
            for k in range(2):
                q[c, 2 * t + k] = v[k * rows : (k + 1) * rows, c * cols : (c + 1) * cols]

    def tile_k(t):
        at, v = projected(1, t)
        for c in range(CHUNKS):
            mine = jnp.concatenate([q[c, 2 * t], q[c, 2 * t + 1]], axis=0).astype(jnp.float32)
            for k in range(cols // 128):
                head = slice(c * cols + k * 128, c * cols + (k + 1) * 128)
                dots = jnp.sum(mine[:, k * 128 : (k + 1) * 128] * v[:, head], axis=-1, keepdims=True)
                own[at, head] = jnp.broadcast_to(silu(alpha * dots), (256, 128))

    def tile_v(t):
        at, v = projected(2, t)
        own[at, :] = own[at, :] * v

    def tile_u(t):
        at, v = projected(3, t)
        gate[at, :] = v

    def q_copy(c, k):
        way, held = GROUPS[k]
        span = pl.ds(STARTS[k], len(held))
        return pltpu.make_async_remote_copy(
            src_ref=qs.at[c, span], dst_ref=qr.at[c, span], send_sem=qss.at[c, k], recv_sem=qrs.at[c, k],
            device_id=(g, plane(turn(way, c))), device_id_type=MESH,
        )

    def r_copy(c, k):
        way, held = GROUPS[k]
        dy, dx = turn(way, c)
        return pltpu.make_async_remote_copy(
            src_ref=res.at[c, pl.ds(STARTS[k], len(held))],
            dst_ref=mix.at[c, pl.ds(HERE + STARTS[k], len(held))],
            send_sem=rss.at[c, k], recv_sem=rrs.at[c, k],
            device_id=(g, plane((-dy, -dx))), device_id_type=MESH,
        )

    def ask():
        @pl.loop(0, CHUNKS)
        def _(c):
            for k, (_, held) in enumerate(GROUPS):
                for n in range(len(held)):
                    at = STARTS[k] + n
                    qs[c, at] = q[c, block_of[user_of(c, HERE + at)]]
            for k in range(len(GROUPS)):
                q_copy(c, k).start()

    def attend(c):
        for k in range(len(GROUPS)):
            q_copy(c, k).wait_recv()
        for held in range(HERE):
            from_here = q[c, block_of[user_of(c, held)]]
            others = [p for p, (_, at) in enumerate(SENT) if at == held]
            rows_in = jnp.concatenate([from_here] + [qr[c, p] for p in others], axis=0)
            for k in range(cols // 128):
                head = slice(k * 128, (k + 1) * 128)
                raw = lax.dot_general(
                    rows_in[:, head], kv[c, held, 0:256, head], (((1,), (1,)), ((), ())),
                    preferred_element_type=jnp.float32,
                )
                weight = silu(alpha * raw).astype(jnp.bfloat16)
                out = jnp.dot(weight, kv[c, held, 256:512, head], preferred_element_type=jnp.float32)
                out = out.astype(jnp.bfloat16)
                mix[c, held, :, head] = out[0:rows]
                for n, p in enumerate(others):
                    res[c, p, :, head] = out[(n + 1) * rows : (n + 2) * rows]
        for k in range(len(GROUPS)):
            r_copy(c, k).start()

    def leaves(c):
        for child in range(1, HERE):
            if child not in PARENT:
                kv_send(c, child).wait_recv()

    tiles = (None, tile_q, tile_k, tile_v, tile_u)
    for j in range(5):

        @pl.loop(0, 4)
        def _(t):
            tick(j, t)
            if tiles[j] is not None:
                tiles[j](t)

        p_wait(j)
        if j == 0:
            kv_level(1, None)
        if j == 1:
            ask()
            kv_level(2, None)
        if j == 2:
            for c in range(CHUNKS):
                leaves(c)
            pl.loop(0, 2)(attend)
        if j == 3:
            pl.loop(2, 4)(attend)

    for c in range(CHUNKS):
        for k in range(len(GROUPS)):
            r_copy(c, k).wait_recv()

    one = lax.broadcasted_iota(jnp.int32, (rows, rows), 0) == lax.broadcasted_iota(jnp.int32, (rows, rows), 1)
    lane = lax.broadcasted_iota(jnp.int32, (1, rows), 1)

    @pl.loop(0, blocks // 2)
    def _(t):
        pair = []
        for k in range(2):
            b = 2 * t + k
            at = pl.ds(pl.multiple_of(b * rows, rows), rows)
            prefix = jnp.concatenate(
                [mix[c, place_of[c * 16 + users[b]]] for c in range(CHUNKS)], axis=1
            ).astype(jnp.float32)
            v = centred(prefix + own[at, :]) * gain_mid[...] * gate[at, :]
            pair.append(v.astype(jnp.bfloat16))
        gated = jnp.concatenate(pair, axis=0)
        out = jnp.dot(gated, wfull[4], preferred_element_type=jnp.float32)
        for k in range(2):
            b = 2 * t + k
            v = xb[b].astype(jnp.float32) + out[k * rows : (k + 1) * rows]
            emb[b] = v.astype(jnp.bfloat16)
            line = jnp.sum(centred(v) * score_vec[...], axis=-1, keepdims=True)
            line = jnp.sum(jnp.where(one, jnp.broadcast_to(line, (rows, rows)), 0.0), axis=0, keepdims=True)
            scores[pl.ds(b, 1), :] = jnp.where(lane < live[b], line, 0.0)

    for copy in sent:
        copy.wait_send()
    for j in range(5):
        for unit in range(2):
            for way in range(2):
                for t in range(4 if unit == way else 3):
                    z_copy(j, t, unit, way, z).wait_send()
        for n in range(8):
            p_copy(j, n, z, core).wait_send()
    for c in range(CHUNKS):
        for k in range(len(GROUPS)):
            q_copy(c, k).wait_send()
            r_copy(c, k).wait_send()


def shards(
    candidates, block_user, live_rows, prefix_keys, prefix_values, w_proj, w_out, gain_in, gain_mid, score_vec
):
    blocks, rows, width = candidates.shape
    dma = pltpu.SemaphoreType.DMA
    bf, f32 = jnp.bfloat16, jnp.float32
    cols = width // CHUNKS
    others, groups = len(SENT), len(GROUPS)
    vmem = pl.BlockSpec(memory_space=pltpu.VMEM)
    smem = pl.BlockSpec(memory_space=pltpu.SMEM)
    anywhere = pl.BlockSpec(memory_space=pl.ANY)
    return pl.pallas_call(
        kernel,
        out_shape=(
            jax.ShapeDtypeStruct((blocks, rows, width), bf),
            jax.ShapeDtypeStruct((blocks, rows), f32),
        ),
        in_specs=[anywhere, smem, smem, anywhere, anywhere, anywhere, anywhere, vmem, vmem, vmem],
        out_specs=(vmem, vmem),
        scratch_shapes=[
            pltpu.VMEM((blocks, rows, width), bf),
            pltpu.VMEM((blocks * rows, width), bf),
            pltpu.VMEM((16, 4, 5 * width), bf),
            pltpu.VMEM((5, width, width), bf),
            pltpu.VMEM((CHUNKS, HERE, 512, cols), bf),
            pltpu.VMEM((CHUNKS, blocks, rows, cols), bf),
            pltpu.VMEM((blocks * rows, width), f32),
            pltpu.VMEM((blocks * rows, width), f32),
            pltpu.VMEM((CHUNKS, others, rows, cols), bf),
            pltpu.VMEM((CHUNKS, others, rows, cols), bf),
            pltpu.VMEM((CHUNKS, others, rows, cols), bf),
            pltpu.VMEM((CHUNKS, PAIRS, rows, cols), bf),
            pltpu.SMEM((16,), jnp.int32),
            pltpu.SMEM((CHUNKS * 16,), jnp.int32),
            dma((11,)),
            dma((16,)), dma((16,)),
            dma((5, 16)), dma((5, 16)),
            dma((5, 8)), dma((5, 8)),
            dma((CHUNKS, HERE)), dma((CHUNKS, HERE)),
            dma((CHUNKS, groups)), dma((CHUNKS, groups)),
            dma((CHUNKS, groups)), dma((CHUNKS, groups)),
        ],
        compiler_params=pltpu.CompilerParams(
            collective_id=0, has_side_effects=True, vmem_limit_bytes=62 * 1024 * 1024
        ),
    )(
        candidates, block_user, live_rows, prefix_keys, prefix_values, w_proj, w_out,
        gain_in[None, :], gain_mid[None, :], score_vec[None, :],
    )


def solution(mesh):
    placed = (
        P(("group", "helper"), None, None),
        P(("group", "helper")),
        P(("group", "helper")),
        P(("group", "helper"), None, None),
        P(("group", "helper"), None, None),
        P(("group", "helper"), None),
        P(("group", "helper"), None),
        P(),
        P(),
        P(),
    )
    return jax.shard_map(
        shards,
        mesh=mesh,
        in_specs=placed,
        out_specs=(P(("group", "helper"), None, None), P(("group", "helper"), None)),
        check_vma=False,
    )
```

```python
import functools

import jax
import jax.numpy as jnp
from jax import lax
from jax.experimental import pallas as pl
from jax.experimental.pallas import tpu as pltpu
from jax.sharding import PartitionSpec as P

MESH = pl.DeviceIdType.MESH
HEADS = 8
EPS = 1e-05
CHUNKS = 4
HOLD = ((0, 0), (0, 1), (1, 0), (0, 2), (2, 0), (2, 3))
PARENT = (None, 0, 0, 1, 2, 4)
LEVELS = ((1, 2), (3, 4), (5,))


def split_others():
    ways = ((0, 1), (0, 3), (1, 0), (3, 0))
    groups = {way: [] for way in ways}
    rest = []
    for y in range(4):
        for x in range(4):
            if (y, x) not in HOLD:
                near = {w: (((y + w[0]) % 4), (x + w[1]) % 4) for w in ways}
                rest.append([(w, HOLD.index(n)) for w, n in near.items() if n in HOLD])
    for options in sorted(rest, key=len):
        way, held = min(options, key=lambda o: len(groups[o[0]]))
        groups[way].append(held)
    return tuple((way, tuple(held)) for way, held in groups.items() if held)


GROUPS = split_others()
STARTS = tuple(sum(len(h) for _, h in GROUPS[:k]) for k in range(len(GROUPS)))
SENT = tuple((way, held) for way, helds in GROUPS for held in helds)
HERE = len(HOLD)
UNITS = 2
PAIRS = HERE + len(SENT)


def turn(offset, c):
    dy, dx = offset
    even, odd = (1 - c % 2) * (1 - c), (c % 2) * (2 - c)
    return even * dy + odd * dx, even * dx - odd * dy


def silu(v):
    half = 0.5 * v
    return half + half * jnp.tanh(half)


def centred(v):
    v = v - jnp.mean(v, axis=-1, keepdims=True)
    return v * lax.rsqrt(jnp.mean(v * v, axis=-1, keepdims=True) + EPS)


def kernel(
    cand, users, live, keys, values, w_proj, w_out, gain_in_hbm, gain_mid_hbm, score_vec_hbm,
    emb, scores,
    xb, normed, wraw, wfull, kv, q, own, gate, qs, qr, res, mix, gain_in, gain_mid, score_vec, block_of, place_of,
    loc, w1s, w1r, zs, zr, ps, pr, ks, kr, qss, qrs, rss, rrs,
):
    g, h = lax.axis_index("group"), lax.axis_index("helper")
    z, core = g // 2, g % 2
    y, x = h // 4, h % 4
    blocks, rows, width = xb.shape
    part = wraw.shape[2] // 5
    cols = width // CHUNKS
    alpha = (width // HEADS) ** -0.5

    def plane(offset):
        return lax.rem(y + offset[0] + 8, 4) * 4 + lax.rem(x + offset[1] + 8, 4)

    def along(step):
        return lax.rem(z + step + 8, 8)

    local = [
        pltpu.make_async_copy(
            w_proj.at[:, pl.ds(2 * part, 2 * part)], wraw.at[h, :, pl.ds(0, 2 * part)], loc.at[0]
        ),
        pltpu.make_async_copy(
            w_proj.at[:, pl.ds(0, 2 * part)], wraw.at[h, :, pl.ds(2 * part, 2 * part)], loc.at[1]
        ),
        pltpu.make_async_copy(w_out, wraw.at[h, :, pl.ds(4 * part, part)], loc.at[11]),
        pltpu.make_async_copy(cand, xb, loc.at[2]),
    ]
    for c in range(CHUNKS):
        for k, src in enumerate((keys, values)):
            local.append(
                pltpu.make_async_copy(
                    src.at[0, :, pl.ds(c * cols, cols)],
                    kv.at[c, 0, pl.ds(k * 256, 256)],
                    loc.at[3 + 2 * c + k],
                )
            )
    for k, (src, dst) in enumerate(((gain_in_hbm, gain_in), (gain_mid_hbm, gain_mid), (score_vec_hbm, score_vec))):
        local.append(pltpu.make_async_copy(src, dst, loc.at[12 + k]))
    for copy in local:
        copy.start()

    barrier = pltpu.get_barrier_semaphore()
    peers = [(g, lax.rem(h + k, 16)) for k in range(1, 16)]
    peers += [(2 * along(1) + core, h), (2 * along(-1) + core, h), (2 * z + 1 - core, h)]
    for peer in peers:
        pl.semaphore_signal(barrier, inc=1, device_id=peer, device_id_type=MESH)
    pl.semaphore_wait(barrier, len(peers))

    sent = []

    def send(src, dst, s, r, device):
        copy = pltpu.make_async_remote_copy(
            src_ref=src, dst_ref=dst, send_sem=s, recv_sem=r, device_id=device, device_id_type=MESH
        )
        copy.start()
        return copy

    for copy in local[:3]:
        copy.wait()

    def w1(n, k, at):
        ref = wraw.at[at, :, pl.ds(*((0, part), (part, 4 * part))[n])]
        return pltpu.make_async_remote_copy(
            src_ref=ref, dst_ref=ref, send_sem=w1s.at[n, k], recv_sem=w1r.at[n, k],
            device_id=(g, lax.rem(h + k, 16)), device_id_type=MESH,
        )

    for n in range(2):
        for k in range(1, 16):
            copy = w1(n, k, h)
            copy.start()
            sent.append(copy)

    def kv_send(c, child):
        parent = PARENT[child]
        a, b = HOLD[parent], HOLD[child]
        step = turn((b[0] - a[0], b[1] - a[1]), c)
        step = tuple((s + 2) % 4 - 2 if s not in (2, -2) else s for s in step)
        return pltpu.make_async_remote_copy(
            src_ref=kv.at[c, parent], dst_ref=kv.at[c, child], send_sem=ks.at[c, child],
            recv_sem=kr.at[c, child], device_id=(g, plane(step)), device_id_type=MESH,
        )

    def kv_level(level):
        for c in range(CHUNKS):
            if level == 0:
                local[4 + 2 * c].wait()
                local[5 + 2 * c].wait()
            for child in LEVELS[level]:
                if PARENT[child]:
                    kv_send(c, PARENT[child]).wait_recv()
                copy = kv_send(c, child)
                copy.start()
                sent.append(copy)

    kv_level(0)

    for u in range(16):
        found = jnp.int32(0)
        for b in range(blocks):
            found = jnp.where(users[b] == u, jnp.int32(b), found)
        block_of[u] = found

    def user_of(c, p):
        if p < HERE:
            dy, dx = turn(HOLD[p], c)
            return plane((-dy, -dx))
        way, held = SENT[p - HERE]
        dy, dx = turn((way[0] - HOLD[held][0], way[1] - HOLD[held][1]), c)
        return plane((dy, dx))

    for c in range(CHUNKS):
        for p in range(PAIRS):
            place_of[c * 16 + user_of(c, p)] = jnp.int32(p)

    for k in (3, 12, 13, 14):
        local[k].wait()

    @pl.loop(0, blocks)
    def _(b):
        v = centred(xb[b].astype(jnp.float32)) * gain_in[...]
        normed[pl.ds(pl.multiple_of(b * rows, rows), rows), :] = v.astype(jnp.bfloat16)

    def slab(at, of_core):
        return pl.ds(pl.multiple_of((2 * at + of_core) * 64, 64), 64)

    def z_copy(j, t, unit, way, at):
        ref = wfull.at[j, slab(at, core), pl.ds(unit * (part // UNITS), part // UNITS)]
        where = (t * UNITS + unit) * 2 + way
        return pltpu.make_async_remote_copy(
            src_ref=ref, dst_ref=ref, send_sem=zs.at[j, where], recv_sem=zr.at[j, where],
            device_id=(2 * along(1 - 2 * way) + core, h), device_id_type=MESH,
        )

    def p_copy(j, n, at, of_core):
        ref = wfull.at[j, slab(at, of_core)]
        return pltpu.make_async_remote_copy(
            src_ref=ref, dst_ref=ref, send_sem=ps.at[j, n], recv_sem=pr.at[j, n],
            device_id=(2 * z + 1 - core, h), device_id_type=MESH,
        )

    def z_own(j):
        for unit in range(UNITS):
            for way in range(2):
                z_copy(j, 0, unit, way, z).start()
        p_copy(j, 0, z, core).start()

    def tick(j, t):
        left, right = along(-1 - t), lax.rem(z + 1 + t, 8)
        for unit in range(UNITS):
            for way in range(2):
                at = (left, right)[way]

                def step(last):
                    z_copy(j, t, unit, way, at).wait_recv()

                    @pl.when(t < last)
                    def _():
                        z_copy(j, t + 1, unit, way, at).start()

                if unit % 2 == way:
                    step(3)
                else:
                    pl.when(t < 3)(functools.partial(step, 2))
        p_copy(j, 1 + 2 * t, left, core).start()

        @pl.when(t < 3)
        def _():
            p_copy(j, 2 + 2 * t, right, core).start()

    def p_wait(j):
        p_copy(j, 0, z, 1 - core).wait_recv()

        @pl.loop(0, 4)
        def _(t):
            p_copy(j, 1 + 2 * t, along(-1 - t), 1 - core).wait_recv()

            @pl.when(t < 3)
            def _():
                p_copy(j, 2 + 2 * t, lax.rem(z + 1 + t, 8), 1 - core).wait_recv()

    STANDS = (0, 1, 3, 2, 4)

    def stage_one(n):
        for k in range(1, 16):
            w1(n, k, lax.rem(h - k + 16, 16)).wait_recv()
        for j in ((0,), (1, 2, 3, 4))[n]:
            piece = wraw[:, :, pl.ds(STANDS[j] * part, part)]
            wfull[j, slab(z, core), :] = piece.reshape(64, part)

    stage_one(0)
    z_own(0)

    def projected(j, t):
        at = pl.ds(pl.multiple_of(t * 256, 256), 256)
        return at, silu(jnp.dot(normed[at, :], wfull[j], preferred_element_type=jnp.float32))

    def tile_q(t):
        _, v = projected(0, t)
        v = v.astype(jnp.bfloat16)
        for c in range(CHUNKS):
            for k in range(2):
                q[c, 2 * t + k] = v[k * rows : (k + 1) * rows, c * cols : (c + 1) * cols]

    def tile_k(t):
        at, v = projected(1, t)
        for c in range(CHUNKS):
            mine = jnp.concatenate([q[c, 2 * t], q[c, 2 * t + 1]], axis=0).astype(jnp.float32)
            for k in range(cols // 128):
                head = slice(c * cols + k * 128, c * cols + (k + 1) * 128)
                dots = jnp.sum(mine[:, k * 128 : (k + 1) * 128] * v[:, head], axis=-1, keepdims=True)
                own[at, head] = jnp.broadcast_to(silu(alpha * dots), (256, 128))

    def tile_v(t):
        at, v = projected(2, t)
        own[at, :] = own[at, :] * v

    def tile_u(t):
        at, v = projected(3, t)
        gate[at, :] = v

    def q_copy(c, k):
        way, held = GROUPS[k]
        span = pl.ds(STARTS[k], len(held))
        return pltpu.make_async_remote_copy(
            src_ref=qs.at[c, span], dst_ref=qr.at[c, span], send_sem=qss.at[c, k], recv_sem=qrs.at[c, k],
            device_id=(g, plane(turn(way, c))), device_id_type=MESH,
        )

    def r_copy(c, k):
        way, held = GROUPS[k]
        dy, dx = turn(way, c)
        return pltpu.make_async_remote_copy(
            src_ref=res.at[c, pl.ds(STARTS[k], len(held))],
            dst_ref=mix.at[c, pl.ds(HERE + STARTS[k], len(held))],
            send_sem=rss.at[c, k], recv_sem=rrs.at[c, k],
            device_id=(g, plane((-dy, -dx))), device_id_type=MESH,
        )

    def ask():
        @pl.loop(0, CHUNKS)
        def _(c):
            for k, (_, held) in enumerate(GROUPS):
                for n in range(len(held)):
                    at = STARTS[k] + n
                    qs[c, at] = q[c, block_of[user_of(c, HERE + at)]]
            for k in range(len(GROUPS)):
                q_copy(c, k).start()

    def attend(c):
        for k in range(len(GROUPS)):
            q_copy(c, k).wait_recv()
        for held in range(HERE):
            from_here = q[c, block_of[user_of(c, held)]]
            others = [p for p, (_, at) in enumerate(SENT) if at == held]
            rows_in = jnp.concatenate([from_here] + [qr[c, p] for p in others], axis=0)
            for k in range(cols // 128):
                head = slice(k * 128, (k + 1) * 128)
                raw = lax.dot_general(
                    rows_in[:, head], kv[c, held, 0:256, head], (((1,), (1,)), ((), ())),
                    preferred_element_type=jnp.float32,
                )
                weight = silu(alpha * raw).astype(jnp.bfloat16)
                out = jnp.dot(weight, kv[c, held, 256:512, head], preferred_element_type=jnp.float32)
                out = out.astype(jnp.bfloat16)
                mix[c, held, :, head] = out[0:rows]
                for n, p in enumerate(others):
                    res[c, p, :, head] = out[(n + 1) * rows : (n + 2) * rows]
        for k in range(len(GROUPS)):
            r_copy(c, k).start()

    def leaves(c):
        for child in range(1, HERE):
            if child not in PARENT:
                kv_send(c, child).wait_recv()

    tiles = (None, tile_k, tile_v, tile_u)
    for j in range(6):

        def step(half):
            if j > 0:
                tick(j - 1, 2 + half)
            if j < 5:
                tick(j, half)
            if 0 < j < 4:

                @pl.when(half == 0)
                def _():
                    z_own(j + 1)

            if j > 2:
                pl.loop(2 * half, 2 * half + 2)(tiles[j - 2])
            if j in (3, 4):
                attend(2 * (j - 3) + half)

        if j == 0:
            step(0)
            stage_one(1)
            z_own(1)
            step(1)
            continue
        if j == 1:
            step(0)
            kv_level(1)
            step(1)
            p_wait(0)
            pl.loop(0, 4)(tile_q)
            kv_level(2)
            ask()
            continue
        pl.loop(0, 2)(step)
        p_wait(j - 1)
        if j == 2:
            for c in range(CHUNKS):
                leaves(c)

    for c in range(CHUNKS):
        for k in range(len(GROUPS)):
            r_copy(c, k).wait_recv()

    one = lax.broadcasted_iota(jnp.int32, (rows, rows), 0) == lax.broadcasted_iota(jnp.int32, (rows, rows), 1)
    lane = lax.broadcasted_iota(jnp.int32, (1, rows), 1)

    @pl.loop(0, blocks // 2)
    def _(t):
        pair = []
        for k in range(2):
            b = 2 * t + k
            at = pl.ds(pl.multiple_of(b * rows, rows), rows)
            prefix = jnp.concatenate(
                [mix[c, place_of[c * 16 + users[b]]] for c in range(CHUNKS)], axis=1
            ).astype(jnp.float32)
            v = centred(prefix + own[at, :]) * gain_mid[...] * gate[at, :]
            pair.append(v.astype(jnp.bfloat16))
        gated = jnp.concatenate(pair, axis=0)
        out = jnp.dot(gated, wfull[4], preferred_element_type=jnp.float32)
        for k in range(2):
            b = 2 * t + k
            v = xb[b].astype(jnp.float32) + out[k * rows : (k + 1) * rows]
            emb[b] = v.astype(jnp.bfloat16)
            line = jnp.sum(centred(v) * score_vec[...], axis=-1, keepdims=True)
            line = jnp.sum(jnp.where(one, jnp.broadcast_to(line, (rows, rows)), 0.0), axis=0, keepdims=True)
            scores[pl.ds(b, 1), :] = jnp.where(lane < live[b], line, 0.0)

    for copy in sent:
        copy.wait_send()
    for j in range(5):
        for unit in range(UNITS):
            for way in range(2):
                for t in range(4 if unit % 2 == way else 3):
                    z_copy(j, t, unit, way, z).wait_send()
        for n in range(8):
            p_copy(j, n, z, core).wait_send()
    for c in range(CHUNKS):
        for k in range(len(GROUPS)):
            q_copy(c, k).wait_send()
            r_copy(c, k).wait_send()


def shards(
    candidates, block_user, live_rows, prefix_keys, prefix_values, w_proj, w_out, gain_in, gain_mid, score_vec
):
    blocks, rows, width = candidates.shape
    dma = pltpu.SemaphoreType.DMA
    bf, f32 = jnp.bfloat16, jnp.float32
    cols = width // CHUNKS
    others, groups = len(SENT), len(GROUPS)
    vmem = pl.BlockSpec(memory_space=pltpu.VMEM)
    smem = pl.BlockSpec(memory_space=pltpu.SMEM)
    stay = functools.partial(pltpu.with_memory_space_constraint, memory_space=pltpu.HBM)
    anywhere = pl.BlockSpec(memory_space=pl.ANY)
    return pl.pallas_call(
        kernel,
        out_shape=(
            jax.ShapeDtypeStruct((blocks, rows, width), bf),
            jax.ShapeDtypeStruct((blocks, rows), f32),
        ),
        in_specs=[anywhere, smem, smem] + [anywhere] * 7,
        out_specs=(vmem, vmem),
        scratch_shapes=[
            pltpu.VMEM((blocks, rows, width), bf),
            pltpu.VMEM((blocks * rows, width), bf),
            pltpu.VMEM((16, 4, 5 * width), bf),
            pltpu.VMEM((5, width, width), bf),
            pltpu.VMEM((CHUNKS, HERE, 512, cols), bf),
            pltpu.VMEM((CHUNKS, blocks, rows, cols), bf),
            pltpu.VMEM((blocks * rows, width), f32),
            pltpu.VMEM((blocks * rows, width), f32),
            pltpu.VMEM((CHUNKS, others, rows, cols), bf),
            pltpu.VMEM((CHUNKS, others, rows, cols), bf),
            pltpu.VMEM((CHUNKS, others, rows, cols), bf),
            pltpu.VMEM((CHUNKS, PAIRS, rows, cols), bf),
            pltpu.VMEM((1, width), f32),
            pltpu.VMEM((1, width), f32),
            pltpu.VMEM((1, width), f32),
            pltpu.SMEM((16,), jnp.int32),
            pltpu.SMEM((CHUNKS * 16,), jnp.int32),
            dma((15,)),
            dma((2, 16)), dma((2, 16)),
            dma((5, 8 * UNITS)), dma((5, 8 * UNITS)),
            dma((5, 8)), dma((5, 8)),
            dma((CHUNKS, HERE)), dma((CHUNKS, HERE)),
            dma((CHUNKS, groups)), dma((CHUNKS, groups)),
            dma((CHUNKS, groups)), dma((CHUNKS, groups)),
        ],
        compiler_params=pltpu.CompilerParams(
            collective_id=0, has_side_effects=True, vmem_limit_bytes=48 * 1024 * 1024
        ),
    )(
        stay(candidates), stay(block_user), stay(live_rows), stay(prefix_keys), stay(prefix_values), stay(w_proj), stay(w_out),
        stay(gain_in[None, :]), stay(gain_mid[None, :]), stay(score_vec[None, :]),
    )


def solution(mesh):
    placed = (
        P(("group", "helper"), None, None),
        P(("group", "helper")),
        P(("group", "helper")),
        P(("group", "helper"), None, None),
        P(("group", "helper"), None, None),
        P(("group", "helper"), None),
        P(("group", "helper"), None),
        P(),
        P(),
        P(),
    )
    return jax.shard_map(
        shards,
        mesh=mesh,
        in_specs=placed,
        out_specs=(P(("group", "helper"), None, None), P(("group", "helper"), None)),
        check_vma=False,
    )
```

```python
import functools

import jax
import jax.numpy as jnp
from jax import lax
from jax.experimental import pallas as pl
from jax.experimental.pallas import tpu as pltpu
from jax.sharding import PartitionSpec as P

MESH = pl.DeviceIdType.MESH
HEADS = 8
EPS = 1e-05
CHUNKS = 4
HOLD = ((0, 0), (0, 1), (1, 0), (0, 2), (2, 0), (2, 3))
PARENT = (None, 0, 0, 1, 2, 4)
LEVELS = ((1, 2), (3, 4), (5,))


def split_others():
    ways = ((0, 1), (0, 3), (1, 0), (3, 0))
    groups = {way: [] for way in ways}
    rest = []
    for y in range(4):
        for x in range(4):
            if (y, x) not in HOLD:
                near = {w: (((y + w[0]) % 4), (x + w[1]) % 4) for w in ways}
                rest.append([(w, HOLD.index(n)) for w, n in near.items() if n in HOLD])
    for options in sorted(rest, key=len):
        way, held = min(options, key=lambda o: len(groups[o[0]]))
        groups[way].append(held)
    return tuple((way, tuple(held)) for way, held in groups.items() if held)


GROUPS = split_others()
STARTS = tuple(sum(len(h) for _, h in GROUPS[:k]) for k in range(len(GROUPS)))
SENT = tuple((way, held) for way, helds in GROUPS for held in helds)
HERE = len(HOLD)
FIRST, SECOND = (0, 2), (1, 3)
STARTS_AT = (0, 1, 3, 4, 6)
UNITS = 2
PAIRS = HERE + len(SENT)


def turn(offset, c):
    dy, dx = offset
    even, odd = (1 - c % 2) * (1 - c), (c % 2) * (2 - c)
    return even * dy + odd * dx, even * dx - odd * dy


def silu(v):
    half = 0.5 * v
    return half + half * jnp.tanh(half)


def centred(v):
    v = v - jnp.mean(v, axis=-1, keepdims=True)
    return v * lax.rsqrt(jnp.mean(v * v, axis=-1, keepdims=True) + EPS)


def kernel(
    cand, users, live, keys, values, w_proj, w_out, gain_in_hbm, gain_mid_hbm, score_vec_hbm,
    emb, scores,
    xb, normed, wraw, wfull, kv, q, own, gate, qs, qr, res, mix, gain_in, gain_mid, score_vec, block_of, place_of,
    loc, w1s, w1r, zs, zr, ps, pr, ks, kr, qss, qrs, rss, rrs,
):
    g, h = lax.axis_index("group"), lax.axis_index("helper")
    z, core = g // 2, g % 2
    y, x = h // 4, h % 4
    blocks, rows, width = xb.shape
    part = wraw.shape[2] // 5
    cols = width // CHUNKS
    alpha = (width // HEADS) ** -0.5

    def plane(offset):
        return lax.rem(y + offset[0] + 8, 4) * 4 + lax.rem(x + offset[1] + 8, 4)

    def along(step):
        return lax.rem(z + step + 8, 8)

    local = [
        pltpu.make_async_copy(
            w_proj.at[:, pl.ds(2 * part, 2 * part)], wraw.at[h, :, pl.ds(0, 2 * part)], loc.at[0]
        ),
        pltpu.make_async_copy(
            w_proj.at[:, pl.ds(0, 2 * part)], wraw.at[h, :, pl.ds(2 * part, 2 * part)], loc.at[1]
        ),
        pltpu.make_async_copy(w_out, wraw.at[h, :, pl.ds(4 * part, part)], loc.at[11]),
        pltpu.make_async_copy(cand, xb, loc.at[2]),
    ]
    for c in range(CHUNKS):
        for k, src in enumerate((keys, values)):
            local.append(
                pltpu.make_async_copy(
                    src.at[0, :, pl.ds(c * cols, cols)],
                    kv.at[c, 0, pl.ds(k * 256, 256)],
                    loc.at[3 + 2 * c + k],
                )
            )
    for k, (src, dst) in enumerate(((gain_in_hbm, gain_in), (gain_mid_hbm, gain_mid), (score_vec_hbm, score_vec))):
        local.append(pltpu.make_async_copy(src, dst, loc.at[12 + k]))
    for copy in local:
        copy.start()

    barrier = pltpu.get_barrier_semaphore()
    peers = [(g, lax.rem(h + k, 16)) for k in range(1, 16)]
    peers += [(2 * along(1) + core, h), (2 * along(-1) + core, h), (2 * z + 1 - core, h)]
    for peer in peers:
        pl.semaphore_signal(barrier, inc=1, device_id=peer, device_id_type=MESH)
    pl.semaphore_wait(barrier, len(peers))

    sent = []

    def send(src, dst, s, r, device):
        copy = pltpu.make_async_remote_copy(
            src_ref=src, dst_ref=dst, send_sem=s, recv_sem=r, device_id=device, device_id_type=MESH
        )
        copy.start()
        return copy

    for copy in local[:3]:
        copy.wait()

    def w1(n, k, at):
        ref = wraw.at[at, :, pl.ds(*((0, part), (part, 4 * part))[n])]
        return pltpu.make_async_remote_copy(
            src_ref=ref, dst_ref=ref, send_sem=w1s.at[n, k], recv_sem=w1r.at[n, k],
            device_id=(g, lax.rem(h + k, 16)), device_id_type=MESH,
        )

    for n in range(2):
        for k in range(1, 16):
            copy = w1(n, k, h)
            copy.start()
            sent.append(copy)

    def kv_send(c, child):
        parent = PARENT[child]
        a, b = HOLD[parent], HOLD[child]
        step = turn((b[0] - a[0], b[1] - a[1]), c)
        step = tuple((s + 2) % 4 - 2 if s not in (2, -2) else s for s in step)
        return pltpu.make_async_remote_copy(
            src_ref=kv.at[c, parent], dst_ref=kv.at[c, child], send_sem=ks.at[c, child],
            recv_sem=kr.at[c, child], device_id=(g, plane(step)), device_id_type=MESH,
        )

    def kv_level(level, chunks):
        for c in chunks:
            if level == 0:
                local[4 + 2 * c].wait()
                local[5 + 2 * c].wait()
            for child in LEVELS[level]:
                if PARENT[child]:
                    kv_send(c, PARENT[child]).wait_recv()
                copy = kv_send(c, child)
                copy.start()
                sent.append(copy)

    kv_level(0, FIRST + SECOND)

    for u in range(16):
        found = jnp.int32(0)
        for b in range(blocks):
            found = jnp.where(users[b] == u, jnp.int32(b), found)
        block_of[u] = found

    def user_of(c, p):
        if p < HERE:
            dy, dx = turn(HOLD[p], c)
            return plane((-dy, -dx))
        way, held = SENT[p - HERE]
        dy, dx = turn((way[0] - HOLD[held][0], way[1] - HOLD[held][1]), c)
        return plane((dy, dx))

    for c in range(CHUNKS):
        for p in range(PAIRS):
            place_of[c * 16 + user_of(c, p)] = jnp.int32(p)

    for k in (3, 12, 13, 14):
        local[k].wait()

    @pl.loop(0, blocks)
    def _(b):
        v = centred(xb[b].astype(jnp.float32)) * gain_in[...]
        normed[pl.ds(pl.multiple_of(b * rows, rows), rows), :] = v.astype(jnp.bfloat16)

    def slab(at, of_core):
        return pl.ds(pl.multiple_of((2 * at + of_core) * 64, 64), 64)

    def z_copy(j, t, unit, way, at):
        ref = wfull.at[j, slab(at, core), pl.ds(unit * (part // UNITS), part // UNITS)]
        where = (t * UNITS + unit) * 2 + way
        return pltpu.make_async_remote_copy(
            src_ref=ref, dst_ref=ref, send_sem=zs.at[j, where], recv_sem=zr.at[j, where],
            device_id=(2 * along(1 - 2 * way) + core, h), device_id_type=MESH,
        )

    def p_copy(j, n, at, of_core):
        ref = wfull.at[j, slab(at, of_core)]
        return pltpu.make_async_remote_copy(
            src_ref=ref, dst_ref=ref, send_sem=ps.at[j, n], recv_sem=pr.at[j, n],
            device_id=(2 * z + 1 - core, h), device_id_type=MESH,
        )

    def z_own(j):
        for unit in range(UNITS):
            for way in range(2):
                z_copy(j, 0, unit, way, z).start()
        p_copy(j, 0, z, core).start()

    def tick(j, t):
        left, right = along(-1 - t), lax.rem(z + 1 + t, 8)
        for unit in range(UNITS):
            for way in range(2):
                at = (left, right)[way]

                def step(last):
                    z_copy(j, t, unit, way, at).wait_recv()

                    @pl.when(t < last)
                    def _():
                        z_copy(j, t + 1, unit, way, at).start()

                if unit % 2 == way:
                    step(3)
                else:
                    pl.when(t < 3)(functools.partial(step, 2))
        p_copy(j, 1 + 2 * t, left, core).start()

        @pl.when(t < 3)
        def _():
            p_copy(j, 2 + 2 * t, right, core).start()

    def p_wait(j):
        p_copy(j, 0, z, 1 - core).wait_recv()

        @pl.loop(0, 4)
        def _(t):
            p_copy(j, 1 + 2 * t, along(-1 - t), 1 - core).wait_recv()

            @pl.when(t < 3)
            def _():
                p_copy(j, 2 + 2 * t, lax.rem(z + 1 + t, 8), 1 - core).wait_recv()

    STANDS = (0, 1, 3, 2, 4)

    def stage_one(n):
        for k in range(1, 16):
            w1(n, k, lax.rem(h - k + 16, 16)).wait_recv()
        for j in ((0,), (1, 2, 3, 4))[n]:
            piece = wraw[:, :, pl.ds(STANDS[j] * part, part)]
            wfull[j, slab(z, core), :] = piece.reshape(64, part)

    stage_one(0)
    z_own(0)

    def projected(j, t):
        at = pl.ds(pl.multiple_of(t * 256, 256), 256)
        return at, silu(jnp.dot(normed[at, :], wfull[j], preferred_element_type=jnp.float32))

    def tile_q(t):
        _, v = projected(0, t)
        v = v.astype(jnp.bfloat16)
        for c in range(CHUNKS):
            for k in range(2):
                q[c, 2 * t + k] = v[k * rows : (k + 1) * rows, c * cols : (c + 1) * cols]

    def tile_k(t):
        at, v = projected(1, t)
        for c in range(CHUNKS):
            mine = jnp.concatenate([q[c, 2 * t], q[c, 2 * t + 1]], axis=0).astype(jnp.float32)
            for k in range(cols // 128):
                head = slice(c * cols + k * 128, c * cols + (k + 1) * 128)
                dots = jnp.sum(mine[:, k * 128 : (k + 1) * 128] * v[:, head], axis=-1, keepdims=True)
                own[at, head] = jnp.broadcast_to(silu(alpha * dots), (256, 128))

    def tile_v(t):
        at, v = projected(2, t)
        own[at, :] = own[at, :] * v

    def tile_u(t):
        at, v = projected(3, t)
        gate[at, :] = v

    def q_copy(c, k):
        way, held = GROUPS[k]
        span = pl.ds(STARTS[k], len(held))
        return pltpu.make_async_remote_copy(
            src_ref=qs.at[c, span], dst_ref=qr.at[c, span], send_sem=qss.at[c, k], recv_sem=qrs.at[c, k],
            device_id=(g, plane(turn(way, c))), device_id_type=MESH,
        )

    def r_copy(c, k):
        way, held = GROUPS[k]
        dy, dx = turn(way, c)
        return pltpu.make_async_remote_copy(
            src_ref=res.at[c, pl.ds(STARTS[k], len(held))],
            dst_ref=mix.at[c, pl.ds(HERE + STARTS[k], len(held))],
            send_sem=rss.at[c, k], recv_sem=rrs.at[c, k],
            device_id=(g, plane((-dy, -dx))), device_id_type=MESH,
        )

    def ask(chunks):
        @pl.loop(0, len(chunks))
        def _(n):
            c = chunks[0] + 2 * n
            for k, (_, held) in enumerate(GROUPS):
                for m in range(len(held)):
                    at = STARTS[k] + m
                    qs[c, at] = q[c, block_of[user_of(c, HERE + at)]]
            for k in range(len(GROUPS)):
                q_copy(c, k).start()

    def attend(c):
        for k in range(len(GROUPS)):
            q_copy(c, k).wait_recv()
        for held in range(HERE):
            from_here = q[c, block_of[user_of(c, held)]]
            others = [p for p, (_, at) in enumerate(SENT) if at == held]
            rows_in = jnp.concatenate([from_here] + [qr[c, p] for p in others], axis=0)
            for k in range(cols // 128):
                head = slice(k * 128, (k + 1) * 128)
                raw = lax.dot_general(
                    rows_in[:, head], kv[c, held, 0:256, head], (((1,), (1,)), ((), ())),
                    preferred_element_type=jnp.float32,
                )
                weight = silu(alpha * raw).astype(jnp.bfloat16)
                out = jnp.dot(weight, kv[c, held, 256:512, head], preferred_element_type=jnp.float32)
                out = out.astype(jnp.bfloat16)
                mix[c, held, :, head] = out[0:rows]
                for n, p in enumerate(others):
                    res[c, p, :, head] = out[(n + 1) * rows : (n + 2) * rows]
        for k in range(len(GROUPS)):
            r_copy(c, k).start()

    def leaves(c):
        for child in range(1, HERE):
            if child not in PARENT:
                kv_send(c, child).wait_recv()

    def some(work, a, b):
        return lambda: pl.loop(a, b)(work)

    def half(level, chunks):
        return lambda: kv_level(level, chunks)

    def answer(chunks):
        def work():
            for c in chunks:
                leaves(c)
            pl.loop(0, len(chunks))(lambda n: attend(chunks[0] + 2 * n))

        return work

    after = {
        1: (half(1, FIRST),),
        2: (half(1, SECOND),),
        3: (half(2, FIRST), some(tile_q, 0, 4), lambda: ask(FIRST)),
        4: (half(2, SECOND), lambda: ask(SECOND), some(tile_k, 0, 2)),
        5: (some(tile_k, 2, 4),),
        6: (answer(FIRST), some(tile_v, 0, 2)),
        7: (answer(SECOND), some(tile_v, 2, 4)),
        8: (some(tile_u, 0, 2),),
        9: (some(tile_u, 2, 4),),
    }
    for s in range(STARTS_AT[-1] + 4):
        for j, start in enumerate(STARTS_AT):
            if 0 <= s - start < 4:
                tick(j, s - start)
        if s == 0:
            stage_one(1)
        for j, start in enumerate(STARTS_AT):
            if start == s + 1:
                z_own(j)
        for j, start in enumerate(STARTS_AT):
            if start + 3 == s:
                p_wait(j)
        for work in after.get(s, ()):
            work()

    for c in range(CHUNKS):
        for k in range(len(GROUPS)):
            r_copy(c, k).wait_recv()

    one = lax.broadcasted_iota(jnp.int32, (rows, rows), 0) == lax.broadcasted_iota(jnp.int32, (rows, rows), 1)
    lane = lax.broadcasted_iota(jnp.int32, (1, rows), 1)

    def before(t):
        for k in range(2):
            b = 2 * t + k
            at = pl.ds(b * rows, rows)
            prefix = jnp.concatenate(
                [mix[c, place_of[c * 16 + users[b]]] for c in range(CHUNKS)], axis=1
            ).astype(jnp.float32)
            v = centred(prefix + own[at, :]) * gain_mid[...] * gate[at, :]
            normed[at, :] = v.astype(jnp.bfloat16)

    def product(t):
        return jnp.dot(normed[pl.ds(t * 256, 256), :], wfull[4], preferred_element_type=jnp.float32)

    def after_product(t, out):
        for k in range(2):
            b = 2 * t + k
            v = xb[b].astype(jnp.float32) + out[k * rows : (k + 1) * rows]
            emb[b] = v.astype(jnp.bfloat16)
            line = jnp.sum(centred(v) * score_vec[...], axis=-1, keepdims=True)
            line = jnp.sum(jnp.where(one, jnp.broadcast_to(line, (rows, rows)), 0.0), axis=0, keepdims=True)
            scores[pl.ds(b, 1), :] = jnp.where(lane < live[b], line, 0.0)

    before(0)
    for t in range(blocks // 2):
        out = product(t)
        if t + 1 < blocks // 2:
            before(t + 1)
        after_product(t, out)

    for copy in sent:
        copy.wait_send()
    for j in range(5):
        for unit in range(UNITS):
            for way in range(2):
                for t in range(4 if unit % 2 == way else 3):
                    z_copy(j, t, unit, way, z).wait_send()
        for n in range(8):
            p_copy(j, n, z, core).wait_send()
    for c in range(CHUNKS):
        for k in range(len(GROUPS)):
            q_copy(c, k).wait_send()
            r_copy(c, k).wait_send()


def shards(
    candidates, block_user, live_rows, prefix_keys, prefix_values, w_proj, w_out, gain_in, gain_mid, score_vec
):
    blocks, rows, width = candidates.shape
    dma = pltpu.SemaphoreType.DMA
    bf, f32 = jnp.bfloat16, jnp.float32
    cols = width // CHUNKS
    others, groups = len(SENT), len(GROUPS)
    vmem = pl.BlockSpec(memory_space=pltpu.VMEM)
    smem = pl.BlockSpec(memory_space=pltpu.SMEM)
    stay = functools.partial(pltpu.with_memory_space_constraint, memory_space=pltpu.HBM)
    anywhere = pl.BlockSpec(memory_space=pl.ANY)
    return pl.pallas_call(
        kernel,
        out_shape=(
            jax.ShapeDtypeStruct((blocks, rows, width), bf),
            jax.ShapeDtypeStruct((blocks, rows), f32),
        ),
        in_specs=[anywhere, smem, smem] + [anywhere] * 7,
        out_specs=(vmem, vmem),
        scratch_shapes=[
            pltpu.VMEM((blocks, rows, width), bf),
            pltpu.VMEM((blocks * rows, width), bf),
            pltpu.VMEM((16, 4, 5 * width), bf),
            pltpu.VMEM((5, width, width), bf),
            pltpu.VMEM((CHUNKS, HERE, 512, cols), bf),
            pltpu.VMEM((CHUNKS, blocks, rows, cols), bf),
            pltpu.VMEM((blocks * rows, width), f32),
            pltpu.VMEM((blocks * rows, width), f32),
            pltpu.VMEM((CHUNKS, others, rows, cols), bf),
            pltpu.VMEM((CHUNKS, others, rows, cols), bf),
            pltpu.VMEM((CHUNKS, others, rows, cols), bf),
            pltpu.VMEM((CHUNKS, PAIRS, rows, cols), bf),
            pltpu.VMEM((1, width), f32),
            pltpu.VMEM((1, width), f32),
            pltpu.VMEM((1, width), f32),
            pltpu.SMEM((16,), jnp.int32),
            pltpu.SMEM((CHUNKS * 16,), jnp.int32),
            dma((15,)),
            dma((2, 16)), dma((2, 16)),
            dma((5, 8 * UNITS)), dma((5, 8 * UNITS)),
            dma((5, 8)), dma((5, 8)),
            dma((CHUNKS, HERE)), dma((CHUNKS, HERE)),
            dma((CHUNKS, groups)), dma((CHUNKS, groups)),
            dma((CHUNKS, groups)), dma((CHUNKS, groups)),
        ],
        compiler_params=pltpu.CompilerParams(
            collective_id=0, has_side_effects=True, vmem_limit_bytes=48 * 1024 * 1024
        ),
    )(
        stay(candidates), stay(block_user), stay(live_rows), stay(prefix_keys), stay(prefix_values), stay(w_proj), stay(w_out),
        stay(gain_in[None, :]), stay(gain_mid[None, :]), stay(score_vec[None, :]),
    )


def solution(mesh):
    placed = (
        P(("group", "helper"), None, None),
        P(("group", "helper")),
        P(("group", "helper")),
        P(("group", "helper"), None, None),
        P(("group", "helper"), None, None),
        P(("group", "helper"), None),
        P(("group", "helper"), None),
        P(),
        P(),
        P(),
    )
    return jax.shard_map(
        shards,
        mesh=mesh,
        in_specs=placed,
        out_specs=(P(("group", "helper"), None, None), P(("group", "helper"), None)),
        check_vma=False,
    )
```

```python
import functools

import jax
import jax.numpy as jnp
from jax import lax
from jax.experimental import pallas as pl
from jax.experimental.pallas import tpu as pltpu
from jax.sharding import PartitionSpec as P

MESH = pl.DeviceIdType.MESH
HEADS = 8
EPS = 1e-05
CHUNKS = 4
HOLD = ((0, 0), (0, 1), (1, 0), (0, 2), (2, 0), (2, 3))
PARENT = (None, 0, 0, 1, 2, 4)
LEVELS = ((1, 2), (3, 4), (5,))


def split_others():
    ways = ((0, 1), (0, 3), (1, 0), (3, 0))
    groups = {way: [] for way in ways}
    rest = []
    for y in range(4):
        for x in range(4):
            if (y, x) not in HOLD:
                near = {w: (((y + w[0]) % 4), (x + w[1]) % 4) for w in ways}
                rest.append([(w, HOLD.index(n)) for w, n in near.items() if n in HOLD])
    for options in sorted(rest, key=len):
        way, held = min(options, key=lambda o: len(groups[o[0]]))
        groups[way].append(held)
    return tuple((way, tuple(held)) for way, held in groups.items() if held)


GROUPS = split_others()
STARTS = tuple(sum(len(h) for _, h in GROUPS[:k]) for k in range(len(GROUPS)))
SENT = tuple((way, held) for way, helds in GROUPS for held in helds)
HERE = len(HOLD)
FIRST, SECOND = (0, 2), (1, 3)
STARTS_AT = (0, 1, 3, 4, 5)
UNITS = 2
PAIRS = HERE + len(SENT)


def turn(offset, c):
    dy, dx = offset
    even, odd = (1 - c % 2) * (1 - c), (c % 2) * (2 - c)
    return even * dy + odd * dx, even * dx - odd * dy


def silu(v):
    half = 0.5 * v
    return half + half * jnp.tanh(half)


def centred(v):
    v = v - jnp.mean(v, axis=-1, keepdims=True)
    return v * lax.rsqrt(jnp.mean(v * v, axis=-1, keepdims=True) + EPS)


def kernel(
    cand, users, live, keys, values, w_proj, w_out, gain_in_hbm, gain_mid_hbm, score_vec_hbm,
    emb, scores,
    xb, normed, wraw, wfull, kv, q, own, gate, qs, qr, res, mix, gain_in, gain_mid, score_vec, block_of, place_of,
    loc, w1s, w1r, zs, zr, ps, pr, ks, kr, qss, qrs, rss, rrs,
):
    g, h = lax.axis_index("group"), lax.axis_index("helper")
    z, core = g // 2, g % 2
    y, x = h // 4, h % 4
    blocks, rows, width = xb.shape
    part = wraw.shape[2] // 5
    cols = width // CHUNKS
    alpha = (width // HEADS) ** -0.5

    def plane(offset):
        return lax.rem(y + offset[0] + 8, 4) * 4 + lax.rem(x + offset[1] + 8, 4)

    def along(step):
        return lax.rem(z + step + 8, 8)

    local = [
        pltpu.make_async_copy(
            w_proj.at[:, pl.ds(2 * part, 2 * part)], wraw.at[h, :, pl.ds(0, 2 * part)], loc.at[0]
        ),
        pltpu.make_async_copy(
            w_proj.at[:, pl.ds(0, 2 * part)], wraw.at[h, :, pl.ds(2 * part, 2 * part)], loc.at[1]
        ),
        pltpu.make_async_copy(w_out, wraw.at[h, :, pl.ds(4 * part, part)], loc.at[11]),
        pltpu.make_async_copy(cand, xb, loc.at[2]),
    ]
    for c in range(CHUNKS):
        for k, src in enumerate((keys, values)):
            local.append(
                pltpu.make_async_copy(
                    src.at[0, :, pl.ds(c * cols, cols)],
                    kv.at[c, 0, pl.ds(k * 256, 256)],
                    loc.at[3 + 2 * c + k],
                )
            )
    for k, (src, dst) in enumerate(((gain_in_hbm, gain_in), (gain_mid_hbm, gain_mid), (score_vec_hbm, score_vec))):
        local.append(pltpu.make_async_copy(src, dst, loc.at[12 + k]))
    for copy in local:
        copy.start()

    barrier = pltpu.get_barrier_semaphore()
    peers = [(g, lax.rem(h + k, 16)) for k in range(1, 16)]
    peers += [(2 * along(1) + core, h), (2 * along(-1) + core, h), (2 * z + 1 - core, h)]
    for peer in peers:
        pl.semaphore_signal(barrier, inc=1, device_id=peer, device_id_type=MESH)
    pl.semaphore_wait(barrier, len(peers))

    sent = []

    def send(src, dst, s, r, device):
        copy = pltpu.make_async_remote_copy(
            src_ref=src, dst_ref=dst, send_sem=s, recv_sem=r, device_id=device, device_id_type=MESH
        )
        copy.start()
        return copy

    for copy in local[:3]:
        copy.wait()

    def w1(n, k, at):
        ref = wraw.at[at, :, pl.ds(*((0, part), (part, 4 * part))[n])]
        return pltpu.make_async_remote_copy(
            src_ref=ref, dst_ref=ref, send_sem=w1s.at[n, k], recv_sem=w1r.at[n, k],
            device_id=(g, lax.rem(h + k, 16)), device_id_type=MESH,
        )

    for n in range(2):
        for k in range(1, 16):
            copy = w1(n, k, h)
            copy.start()
            sent.append(copy)

    def kv_send(c, child):
        parent = PARENT[child]
        a, b = HOLD[parent], HOLD[child]
        step = turn((b[0] - a[0], b[1] - a[1]), c)
        step = tuple((s + 2) % 4 - 2 if s not in (2, -2) else s for s in step)
        return pltpu.make_async_remote_copy(
            src_ref=kv.at[c, parent], dst_ref=kv.at[c, child], send_sem=ks.at[c, child],
            recv_sem=kr.at[c, child], device_id=(g, plane(step)), device_id_type=MESH,
        )

    def kv_level(level, chunks):
        for c in chunks:
            if level == 0:
                local[4 + 2 * c].wait()
                local[5 + 2 * c].wait()
            for child in LEVELS[level]:
                if PARENT[child]:
                    kv_send(c, PARENT[child]).wait_recv()
                copy = kv_send(c, child)
                copy.start()
                sent.append(copy)

    kv_level(0, FIRST + SECOND)

    for u in range(16):
        found = jnp.int32(0)
        for b in range(blocks):
            found = jnp.where(users[b] == u, jnp.int32(b), found)
        block_of[u] = found

    def user_of(c, p):
        if p < HERE:
            dy, dx = turn(HOLD[p], c)
            return plane((-dy, -dx))
        way, held = SENT[p - HERE]
        dy, dx = turn((way[0] - HOLD[held][0], way[1] - HOLD[held][1]), c)
        return plane((dy, dx))

    for c in range(CHUNKS):
        for p in range(PAIRS):
            place_of[c * 16 + user_of(c, p)] = jnp.int32(p)

    for k in (3, 12, 13, 14):
        local[k].wait()

    @pl.loop(0, blocks)
    def _(b):
        v = centred(xb[b].astype(jnp.float32)) * gain_in[...]
        normed[pl.ds(pl.multiple_of(b * rows, rows), rows), :] = v.astype(jnp.bfloat16)

    def slab(at, of_core):
        return pl.ds(pl.multiple_of((2 * at + of_core) * 64, 64), 64)

    def z_copy(j, t, unit, way, at):
        ref = wfull.at[j, slab(at, core), pl.ds(unit * (part // UNITS), part // UNITS)]
        where = (t * UNITS + unit) * 2 + way
        return pltpu.make_async_remote_copy(
            src_ref=ref, dst_ref=ref, send_sem=zs.at[j, where], recv_sem=zr.at[j, where],
            device_id=(2 * along(1 - 2 * way) + core, h), device_id_type=MESH,
        )

    def p_copy(j, n, at, of_core):
        ref = wfull.at[j, slab(at, of_core)]
        return pltpu.make_async_remote_copy(
            src_ref=ref, dst_ref=ref, send_sem=ps.at[j, n], recv_sem=pr.at[j, n],
            device_id=(2 * z + 1 - core, h), device_id_type=MESH,
        )

    def z_own(j):
        for unit in range(UNITS):
            for way in range(2):
                z_copy(j, 0, unit, way, z).start()
        p_copy(j, 0, z, core).start()

    def tick(j, t):
        left, right = along(-1 - t), lax.rem(z + 1 + t, 8)
        for unit in range(UNITS):
            for way in range(2):
                at = (left, right)[way]

                def step(last):
                    z_copy(j, t, unit, way, at).wait_recv()

                    @pl.when(t < last)
                    def _():
                        z_copy(j, t + 1, unit, way, at).start()

                if unit % 2 == way:
                    step(3)
                else:
                    pl.when(t < 3)(functools.partial(step, 2))
        p_copy(j, 1 + 2 * t, left, core).start()

        @pl.when(t < 3)
        def _():
            p_copy(j, 2 + 2 * t, right, core).start()

    def p_wait(j):
        p_copy(j, 0, z, 1 - core).wait_recv()

        @pl.loop(0, 4)
        def _(t):
            p_copy(j, 1 + 2 * t, along(-1 - t), 1 - core).wait_recv()

            @pl.when(t < 3)
            def _():
                p_copy(j, 2 + 2 * t, lax.rem(z + 1 + t, 8), 1 - core).wait_recv()

    STANDS = (0, 1, 3, 2, 4)

    def stage_one(n):
        for k in range(1, 16):
            w1(n, k, lax.rem(h - k + 16, 16)).wait_recv()
        for j in ((0,), (1, 2, 3, 4))[n]:
            piece = wraw[:, :, pl.ds(STANDS[j] * part, part)]
            wfull[j, slab(z, core), :] = piece.reshape(64, part)

    stage_one(0)
    z_own(0)

    def projected(j, t):
        at = pl.ds(pl.multiple_of(t * 256, 256), 256)
        return at, silu(jnp.dot(normed[at, :], wfull[j], preferred_element_type=jnp.float32))

    def tile_q(t):
        _, v = projected(0, t)
        v = v.astype(jnp.bfloat16)
        for c in range(CHUNKS):
            for k in range(2):
                q[c, 2 * t + k] = v[k * rows : (k + 1) * rows, c * cols : (c + 1) * cols]

    def tile_k(t):
        at, v = projected(1, t)
        for c in range(CHUNKS):
            mine = jnp.concatenate([q[c, 2 * t], q[c, 2 * t + 1]], axis=0).astype(jnp.float32)
            for k in range(cols // 128):
                head = slice(c * cols + k * 128, c * cols + (k + 1) * 128)
                dots = jnp.sum(mine[:, k * 128 : (k + 1) * 128] * v[:, head], axis=-1, keepdims=True)
                own[at, head] = jnp.broadcast_to(silu(alpha * dots), (256, 128))

    def tile_v(t):
        at, v = projected(2, t)
        own[at, :] = own[at, :] * v

    def tile_u(t):
        at, v = projected(3, t)
        gate[at, :] = v

    def q_copy(c, k):
        way, held = GROUPS[k]
        span = pl.ds(STARTS[k], len(held))
        return pltpu.make_async_remote_copy(
            src_ref=qs.at[c, span], dst_ref=qr.at[c, span], send_sem=qss.at[c, k], recv_sem=qrs.at[c, k],
            device_id=(g, plane(turn(way, c))), device_id_type=MESH,
        )

    def r_copy(c, k):
        way, held = GROUPS[k]
        dy, dx = turn(way, c)
        return pltpu.make_async_remote_copy(
            src_ref=res.at[c, pl.ds(STARTS[k], len(held))],
            dst_ref=mix.at[c, pl.ds(HERE + STARTS[k], len(held))],
            send_sem=rss.at[c, k], recv_sem=rrs.at[c, k],
            device_id=(g, plane((-dy, -dx))), device_id_type=MESH,
        )

    def ask(chunks):
        @pl.loop(0, len(chunks))
        def _(n):
            c = chunks[0] + 2 * n
            for k, (_, held) in enumerate(GROUPS):
                for m in range(len(held)):
                    at = STARTS[k] + m
                    qs[c, at] = q[c, block_of[user_of(c, HERE + at)]]
            for k in range(len(GROUPS)):
                q_copy(c, k).start()

    def attend(c):
        for k in range(len(GROUPS)):
            q_copy(c, k).wait_recv()
        for held in range(HERE):
            from_here = q[c, block_of[user_of(c, held)]]
            others = [p for p, (_, at) in enumerate(SENT) if at == held]
            rows_in = jnp.concatenate([from_here] + [qr[c, p] for p in others], axis=0)
            for k in range(cols // 128):
                head = slice(k * 128, (k + 1) * 128)
                raw = lax.dot_general(
                    rows_in[:, head], kv[c, held, 0:256, head], (((1,), (1,)), ((), ())),
                    preferred_element_type=jnp.float32,
                )
                weight = silu(alpha * raw).astype(jnp.bfloat16)
                out = jnp.dot(weight, kv[c, held, 256:512, head], preferred_element_type=jnp.float32)
                out = out.astype(jnp.bfloat16)
                mix[c, held, :, head] = out[0:rows]
                for n, p in enumerate(others):
                    res[c, p, :, head] = out[(n + 1) * rows : (n + 2) * rows]
        for k in range(len(GROUPS)):
            r_copy(c, k).start()

    def leaves(c):
        for child in range(1, HERE):
            if child not in PARENT:
                kv_send(c, child).wait_recv()

    def some(work, a, b):
        return lambda: pl.loop(a, b)(work)

    def half(level, chunks):
        return lambda: kv_level(level, chunks)

    def whole(j):
        return lambda: p_wait(j)

    def answer(chunks):
        def work():
            for c in chunks:
                leaves(c)
            pl.loop(0, len(chunks))(lambda n: attend(chunks[0] + 2 * n))

        return work

    after = {
        1: (half(1, FIRST),),
        2: (half(1, SECOND),),
        3: (half(2, FIRST), whole(0), some(tile_q, 0, 4), lambda: ask(FIRST)),
        4: (half(2, SECOND), lambda: ask(SECOND)),
        5: (whole(1), some(tile_k, 0, 2)),
        6: (answer(FIRST), some(tile_k, 2, 4)),
        7: (answer(SECOND), whole(2), some(tile_v, 0, 2)),
        8: (some(tile_v, 2, 4), whole(3), some(tile_u, 0, 4), whole(4)),
    }
    for s in range(STARTS_AT[-1] + 4):
        for j, start in enumerate(STARTS_AT):
            if 0 <= s - start < 4:
                tick(j, s - start)
        if s == 0:
            stage_one(1)
        for j, start in enumerate(STARTS_AT):
            if start == s + 1:
                z_own(j)
        for work in after.get(s, ()):
            work()

    for c in range(CHUNKS):
        for k in range(len(GROUPS)):
            r_copy(c, k).wait_recv()

    one = lax.broadcasted_iota(jnp.int32, (rows, rows), 0) == lax.broadcasted_iota(jnp.int32, (rows, rows), 1)
    lane = lax.broadcasted_iota(jnp.int32, (1, rows), 1)

    def before(t):
        for k in range(2):
            b = 2 * t + k
            at = pl.ds(b * rows, rows)
            prefix = jnp.concatenate(
                [mix[c, place_of[c * 16 + users[b]]] for c in range(CHUNKS)], axis=1
            ).astype(jnp.float32)
            v = centred(prefix + own[at, :]) * gain_mid[...] * gate[at, :]
            normed[at, :] = v.astype(jnp.bfloat16)

    def product(t):
        return jnp.dot(normed[pl.ds(t * 256, 256), :], wfull[4], preferred_element_type=jnp.float32)

    def after_product(t, out):
        for k in range(2):
            b = 2 * t + k
            v = xb[b].astype(jnp.float32) + out[k * rows : (k + 1) * rows]
            emb[b] = v.astype(jnp.bfloat16)
            line = jnp.sum(centred(v) * score_vec[...], axis=-1, keepdims=True)
            line = jnp.sum(jnp.where(one, jnp.broadcast_to(line, (rows, rows)), 0.0), axis=0, keepdims=True)
            scores[pl.ds(b, 1), :] = jnp.where(lane < live[b], line, 0.0)

    before(0)
    for t in range(blocks // 2):
        out = product(t)
        if t + 1 < blocks // 2:
            before(t + 1)
        after_product(t, out)

    for copy in sent:
        copy.wait_send()
    for j in range(5):
        for unit in range(UNITS):
            for way in range(2):
                for t in range(4 if unit % 2 == way else 3):
                    z_copy(j, t, unit, way, z).wait_send()
        for n in range(8):
            p_copy(j, n, z, core).wait_send()
    for c in range(CHUNKS):
        for k in range(len(GROUPS)):
            q_copy(c, k).wait_send()
            r_copy(c, k).wait_send()


def shards(
    candidates, block_user, live_rows, prefix_keys, prefix_values, w_proj, w_out, gain_in, gain_mid, score_vec
):
    blocks, rows, width = candidates.shape
    dma = pltpu.SemaphoreType.DMA
    bf, f32 = jnp.bfloat16, jnp.float32
    cols = width // CHUNKS
    others, groups = len(SENT), len(GROUPS)
    vmem = pl.BlockSpec(memory_space=pltpu.VMEM)
    smem = pl.BlockSpec(memory_space=pltpu.SMEM)
    stay = functools.partial(pltpu.with_memory_space_constraint, memory_space=pltpu.HBM)
    anywhere = pl.BlockSpec(memory_space=pl.ANY)
    return pl.pallas_call(
        kernel,
        out_shape=(
            jax.ShapeDtypeStruct((blocks, rows, width), bf),
            jax.ShapeDtypeStruct((blocks, rows), f32),
        ),
        in_specs=[anywhere, smem, smem] + [anywhere] * 7,
        out_specs=(vmem, vmem),
        scratch_shapes=[
            pltpu.VMEM((blocks, rows, width), bf),
            pltpu.VMEM((blocks * rows, width), bf),
            pltpu.VMEM((16, 4, 5 * width), bf),
            pltpu.VMEM((5, width, width), bf),
            pltpu.VMEM((CHUNKS, HERE, 512, cols), bf),
            pltpu.VMEM((CHUNKS, blocks, rows, cols), bf),
            pltpu.VMEM((blocks * rows, width), f32),
            pltpu.VMEM((blocks * rows, width), f32),
            pltpu.VMEM((CHUNKS, others, rows, cols), bf),
            pltpu.VMEM((CHUNKS, others, rows, cols), bf),
            pltpu.VMEM((CHUNKS, others, rows, cols), bf),
            pltpu.VMEM((CHUNKS, PAIRS, rows, cols), bf),
            pltpu.VMEM((1, width), f32),
            pltpu.VMEM((1, width), f32),
            pltpu.VMEM((1, width), f32),
            pltpu.SMEM((16,), jnp.int32),
            pltpu.SMEM((CHUNKS * 16,), jnp.int32),
            dma((15,)),
            dma((2, 16)), dma((2, 16)),
            dma((5, 8 * UNITS)), dma((5, 8 * UNITS)),
            dma((5, 8)), dma((5, 8)),
            dma((CHUNKS, HERE)), dma((CHUNKS, HERE)),
            dma((CHUNKS, groups)), dma((CHUNKS, groups)),
            dma((CHUNKS, groups)), dma((CHUNKS, groups)),
        ],
        compiler_params=pltpu.CompilerParams(
            collective_id=0, has_side_effects=True, vmem_limit_bytes=48 * 1024 * 1024
        ),
    )(
        stay(candidates), stay(block_user), stay(live_rows), stay(prefix_keys), stay(prefix_values), stay(w_proj), stay(w_out),
        stay(gain_in[None, :]), stay(gain_mid[None, :]), stay(score_vec[None, :]),
    )


def solution(mesh):
    placed = (
        P(("group", "helper"), None, None),
        P(("group", "helper")),
        P(("group", "helper")),
        P(("group", "helper"), None, None),
        P(("group", "helper"), None, None),
        P(("group", "helper"), None),
        P(("group", "helper"), None),
        P(),
        P(),
        P(),
    )
    return jax.shard_map(
        shards,
        mesh=mesh,
        in_specs=placed,
        out_specs=(P(("group", "helper"), None, None), P(("group", "helper"), None)),
        check_vma=False,
    )
```
